256 devices in a mesh: dp: 8 (over y, z_hi), mp: 32 (over z_lo, x, core).
Axes of the slice: x: 4, y: 4, z: 8 (z_hi: 2, z_lo: 4; z = z_hi * 4 + z_lo), core: 2. Of those that a mesh axis runs over, the one named last changes fastest.
Arguments:
- features: bfloat16 [256, 1280, 1024], P('dp', 'mp'), may hold values from -6 to 6
- conv_weight: bfloat16 [1280, 1280], P('mp'), may hold values from -0.15625 to 0.15625
- norm_gain: float32 [1280], replicated, may hold values from 0.25 to 1.75
- norm_bias: float32 [1280], replicated, may hold values from -3 to 3
- logit_vector: float32 [1280], replicated, may hold values from -0.625 to 0.625
- labels: int32 [256], P(('dp', 'mp')), may hold values 0 or 1
Outputs:
- grad_features: float32 [256, 1280, 1024], P('dp', 'mp')
- grad_weight: float32 [1280, 1280], P('mp')
- head_grads: float32 [3, 1280], replicated
- loss: float32 [], replicated
The draws below stay inside these ranges and needn't reach their ends.
All inputs are finite; a program needn't handle non-finite values. No bound on the sum of `labels` on one device may be relied on, other than what follows from the above.
Results may differ from the reference program's by a relative error of at most 0.0029.
Values may be sent and summed in bfloat16 or wider, within the bound.
A program may use at most 128 MiB of HBM per device.

```python
import jax
import jax.numpy as jnp
from jax import lax

C = 1280
CELLS = 1024
GROUPS = 32
IMAGES = 256


def plant(values, own_key, low, largest):
    dims = values.shape
    spot = [jax.random.randint(jax.random.fold_in(own_key, axis), (), 0, dims[axis]) for axis in range(len(dims))]
    values = values.at[tuple(spot)].set(low)
    longest = dims.index(max(dims))
    spot[longest] = (spot[longest] + 1) % dims[longest]
    return values.at[tuple(spot)].set(largest)


def levels(own_key, shape, split, smallest, top_value):
    level = 1.0
    for axis_at, shards_of in split:
        steps = jax.random.uniform(jax.random.fold_in(jax.random.fold_in(own_key, 6), axis_at), (shards_of,), jnp.float32, smallest / len(split), top_value / len(split))
        level = level * jnp.repeat(jnp.exp(steps), shape[axis_at] // shards_of).reshape((-1,) + (1,) * (len(shape) - 1 - axis_at))
    return level


def bell_draw(own_key, dims, scale, reach, cuts=(), dtype=jnp.bfloat16):
    result = jax.random.normal(own_key, dims, jnp.float32) * scale
    if len(cuts) > 0:
        result = levels(own_key, dims, cuts, -0.22, 0.18) * result
    return jnp.clip(result, min=-reach, max=reach).astype(dtype)


def setup_inputs(seed: int = 0) -> dict:
    seeds = jax.random.split(jax.random.key(seed), 7)
    return {
        "features": bell_draw(seeds[0], (IMAGES, C, CELLS), 1.0, 6.0, ((0, 8), (1, 32))),
        "conv_weight": bell_draw(seeds[1], (C, C), C ** -0.5, 0.15625, ((0, 32),)),
        "norm_gain": jnp.clip(1.0 + 0.15 * jax.random.normal(seeds[2], (C,), jnp.float32), 0.25, 1.75),
        "norm_bias": bell_draw(seeds[3], (C,), 0.5, 3.0, (), jnp.float32),
        "logit_vector": bell_draw(seeds[4], (C,), (C // 16) ** -0.5, 0.625, (), jnp.float32),
        "labels": plant((jax.random.randint(seeds[5], (IMAGES,), 0, 2) < 1).astype(jnp.int32), jax.random.fold_in(seeds[5], 1), 0, 1),
    }


norm_eps = 1e-05

def head_total(pre, norm_gain, norm_bias, logit_vector, signs):
    images = pre.shape[0]
    grouped = pre.reshape(images, GROUPS, C // GROUPS, CELLS)
    center = lax.optimization_barrier(jnp.mean(grouped, axis=(2, 3), keepdims=True))
    spread = lax.optimization_barrier(jnp.mean((grouped - center) ** 2, axis=(2, 3), keepdims=True))
    normed = ((grouped - center) * lax.rsqrt(spread + norm_eps)).reshape(images, C, CELLS)
    normed = normed * norm_gain[:, None] + norm_bias[:, None]
    hidden = jax.nn.silu(normed)
    logits = jnp.einsum('c,ncs->n', logit_vector, hidden, precision=lax.Precision.HIGHEST) / CELLS
    margin = jnp.maximum(1.0 - signs * logits, 0.0)
    return jnp.sum(margin * margin)

def reference(features, conv_weight, norm_gain, norm_bias, logit_vector, labels):
    weight_wide = conv_weight.astype(jnp.float32)
    signs = 2.0 * labels.astype(jnp.float32) - 1.0

    def one_image(carry, inputs):
        grad_acc, small_acc, total_acc = carry
        image, sign = inputs
        image_wide = image.astype(jnp.float32)
        pre = jnp.einsum('io,is->os', weight_wide, image_wide, precision=lax.Precision.HIGHEST)[None]
        total, pull = jax.vjp(lambda p, g, b, h: head_total(p, g, b, h, sign[None]), pre, norm_gain, norm_bias, logit_vector)
        grad_pre, grad_gain, grad_bias, grad_vec = pull(jnp.ones((), jnp.float32))
        grad_pre = grad_pre[0].astype(jnp.bfloat16).astype(jnp.float32)
        grad_acc = grad_acc + jnp.einsum('is,os->io', image_wide, grad_pre, precision=lax.Precision.HIGHEST)
        grad_image = jnp.einsum('io,os->is', weight_wide, grad_pre, precision=lax.Precision.HIGHEST)
        small_acc = small_acc + jnp.stack([grad_gain, grad_bias, grad_vec])
        return ((grad_acc, small_acc, total_acc + total), grad_image)
    start = (jnp.zeros((C, C), jnp.float32), jnp.zeros((3, C), jnp.float32), jnp.zeros((), jnp.float32))
    (grad_weight, head_grads, total), grad_features = lax.scan(one_image, start, (features, signs))
    loss = total / features.shape[0]
    return (grad_features, grad_weight, head_grads, loss)
```

```python
import jax
import jax.numpy as jnp
from jax import lax
from jax.sharding import Mesh
from jax.sharding import PartitionSpec as P

GROUPS = 32
MP = ("mp_0", "mp_1", "mp_2")
DP = ("dp_0", "dp_1")
DP_MP = ("dp_0", "dp_1", "mp_0", "mp_1", "mp_2")


norm_eps = 1e-05


def from_everyone(x, axis):
    copies = jnp.broadcast_to(x, (lax.axis_size(axis), *x.shape))
    return lax.all_to_all(copies, axis, split_axis=0, concat_axis=0, tiled=True)


def taken_together(x, axis):
    return from_everyone(x, axis).sum(axis=0)


def head_total(pre, norm_gain, norm_bias, logit_vector, signs):
    images, channels, cell_count = pre.shape
    grouped = pre.reshape(images, GROUPS, channels // GROUPS, cell_count)
    center = jnp.mean(grouped, axis=(2, 3), keepdims=True)
    spread = jnp.mean((grouped - center) ** 2, axis=(2, 3), keepdims=True)
    normed = ((grouped - center) * lax.rsqrt(spread + norm_eps)).reshape(
        images, channels, cell_count
    )
    normed = normed * norm_gain[:, None] + norm_bias[:, None]
    hidden = jax.nn.silu(normed)
    logits = (
        jnp.einsum("c,ncs->n", logit_vector, hidden, precision=lax.Precision.HIGHEST) / cell_count
    )
    margin = jnp.maximum(1.0 - signs * logits, 0.0)
    return jnp.sum(margin * margin)


def shards(features, conv_weight, norm_gain, norm_bias, logit_vector, labels):
    signs = 2.0 * labels.astype(jnp.float32) - 1.0
    weight_full = lax.all_gather(conv_weight, MP, axis=0, tiled=True)
    image_block = lax.all_to_all(features, MP, split_axis=0, concat_axis=1, tiled=True)
    pre = jnp.einsum("io,nis->nos", weight_full, image_block, preferred_element_type=jnp.float32)
    total, pull = jax.vjp(
        lambda p, g, b, h: head_total(p, g, b, h, signs), pre, norm_gain, norm_bias, logit_vector
    )
    grad_pre, grad_gain, grad_bias, grad_vec = pull(jnp.ones((), jnp.float32))
    grad_pre = grad_pre.astype(jnp.bfloat16)
    grad_image = jnp.einsum(
        "io,nos->nis", weight_full, grad_pre, preferred_element_type=jnp.float32
    )
    grad_features = lax.all_to_all(
        grad_image.astype(jnp.bfloat16), MP, split_axis=1, concat_axis=0, tiled=True
    ).astype(jnp.float32)
    weight_term = jnp.einsum(
        "nis,nos->io", image_block, grad_pre, preferred_element_type=jnp.float32
    )
    weight_rows = lax.psum_scatter(weight_term, MP, scatter_dimension=0, tiled=True)
    grad_weight = taken_together(weight_rows, DP)
    small = jnp.stack([grad_gain, grad_bias, grad_vec, jnp.full_like(grad_gain, total)])
    small = lax.psum(small, DP_MP)
    total_sum, head_grads = small[3, 0], small[:3]
    image_total = pre.shape[0] * lax.axis_size(DP) * lax.axis_size(MP)
    loss = total_sum / image_total
    return (grad_features, grad_weight, head_grads, loss)


def solution(mesh):
    finer = Mesh(mesh.devices.reshape(4, 2, 4, 4, 2), ("dp_0", "dp_1", "mp_0", "mp_1", "mp_2"))
    placed = (P(DP, MP, None), P(MP, None), P(), P(), P(), P(DP_MP))
    return jax.shard_map(
        shards,
        mesh=finer,
        in_specs=placed,
        out_specs=(P(DP, MP, None), P(MP, None), P(), P()),
        check_vma=False,
    )
```
